128 devices in a mesh: grp: 4 (over z), leaf: 32 (over y, x, core).
Axes of the slice: x: 4, y: 4, z: 4, core: 2. Of those that a mesh axis runs over, the one named last changes fastest.
Arguments:
- matrix: bfloat16 [131072, 512], P(('grp', 'leaf')), may hold values from -6 to 6
- leaf_basis: bfloat16 [131072, 512], P(('grp', 'leaf')), may hold values from -0.1875 to 0.1875
- leaf_tri: bfloat16 [128, 512, 512], P(('grp', 'leaf')), may hold values from -1.5 to 1.5, as said below
- inner_basis: bfloat16 [4, 32, 5, 1024, 512], P('grp', 'leaf'), may hold values from -1 to 1, as said below
- inner_tri: bfloat16 [4, 32, 5, 512, 512], P('grp', 'leaf'), may hold values from -1.5 to 1.5, as said below
- outer_basis: bfloat16 [4, 32, 2, 1024, 512], P('grp', 'leaf'), may hold values from -1 to 1, as said below
- outer_tri: bfloat16 [4, 32, 2, 512, 512], P('grp', 'leaf'), may hold values from -1.5 to 1.5, as said below
Outputs:
- reduced: bfloat16 [512, 512], P(None, ('grp', 'leaf'))
The draws below stay inside these ranges and needn't reach their ends.
Inputs may be any that keep to these rules, and one draw needn't show every extreme that they name: `leaf_tri`: upper triangular; diagonal entries between 0.5 and 1.5. `inner_basis`: equal for all leaves under the same inner node of level l. `inner_tri`: upper triangular, diagonal entries between 0.5 and 1.5; equal for all leaves under the same inner node of level l. `outer_basis`: equal for all leaves under the same outer node of level m. `outer_tri`: upper triangular, diagonal entries between 0.5 and 1.5; equal for all leaves under the same outer node of level m.
All inputs are finite; a program needn't handle non-finite values.
Results may differ from the reference program's by a relative error of at most 0.0045.
Values sent between devices are 32-bit elements; how exact they have to be, the bound alone decides.
No kernel may reach another device: no remote copies, remote signals or barrier semaphores. Data moves between devices by JAX's collectives and lax.ppermute only.
A program may use at most 64 MiB of HBM per device.

```python
import jax
import jax.numpy as jnp
from jax import lax

K = 512
P_SIZE = 512
LEAF_ROWS = 1024
LEAF_DEPTH = 5
GRP_DEPTH = 2
ROWS = 131072
N_GRP = 4
N_LEAF = 32


def rough_values(first_key, shape):
    values = jnp.clip(jax.random.normal(first_key, shape, jnp.float32), -4.0, 4.0)
    return values


def triangle_table(first_key, leading):
    upper_key, diag_key = jax.random.split(first_key)
    upper = rough_values(upper_key, leading + (K, K)) * (0.5 / K ** 0.5)
    diagonal = jax.random.uniform(diag_key, leading + (K,), jnp.float32, 0.5, 1.5)
    strict = jnp.triu(jnp.ones((K, K), jnp.float32), 1)
    return (upper * strict + diagonal[..., None] * jnp.eye(K, dtype=jnp.float32)).astype(jnp.bfloat16)


def basis_table(first_key, leading):
    return (rough_values(first_key, leading + (2 * K, K)) * (2 * K) ** (-0.5)).astype(jnp.bfloat16)


def inner_nodes():
    leaf_ids = jnp.arange(N_LEAF, dtype=jnp.int32)[:, None]
    heights = jnp.arange(LEAF_DEPTH, dtype=jnp.int32)[None, :]
    return (heights, jnp.right_shift(leaf_ids, heights + 1))


def outer_nodes():
    group_ids = jnp.arange(N_GRP, dtype=jnp.int32)[:, None]
    heights = jnp.arange(GRP_DEPTH, dtype=jnp.int32)[None, :]
    return (heights, jnp.right_shift(group_ids, heights + 1))


def draw_leaf_tri(key, part):
    return triangle_table(jax.random.fold_in(key, 11), (N_GRP * N_LEAF,))


def draw_inner_basis(key, part):
    table = basis_table(jax.random.fold_in(key, 21), (N_GRP, LEAF_DEPTH, N_LEAF // 2))
    heights, node_ids = inner_nodes()
    return table[:, heights, node_ids]


def draw_inner_tri(key, part):
    table = triangle_table(jax.random.fold_in(key, 31), (N_GRP, LEAF_DEPTH, N_LEAF // 2))
    heights, node_ids = inner_nodes()
    return table[:, heights, node_ids]


def draw_outer_basis(key, part):
    table = basis_table(jax.random.fold_in(key, 41), (GRP_DEPTH, N_GRP // 2))
    heights, node_ids = outer_nodes()
    picked = table[heights, node_ids]
    return jnp.broadcast_to(picked[:, None], (N_GRP, N_LEAF, GRP_DEPTH, 2 * K, K))


def draw_outer_tri(key, part):
    table = triangle_table(jax.random.fold_in(key, 51), (GRP_DEPTH, N_GRP // 2))
    heights, node_ids = outer_nodes()
    picked = table[heights, node_ids]
    return jnp.broadcast_to(picked[:, None], (N_GRP, N_LEAF, GRP_DEPTH, K, K))


def levels(stream_key, dims, pieces, least, largest):
    loudness = 1.0
    for axis_at, blocks in pieces:
        steps = jax.random.uniform(jax.random.fold_in(jax.random.fold_in(stream_key, 6), axis_at), (blocks,), jnp.float32, least / len(pieces), largest / len(pieces))
        loudness = loudness * jnp.repeat(jnp.exp(steps), dims[axis_at] // blocks).reshape((-1,) + (1,) * (len(dims) - 1 - axis_at))
    return loudness


def noise(key, extent, deviation, most, shards=(), kind=jnp.bfloat16):
    drawn = deviation * jax.random.normal(key, extent, jnp.float32)
    if shards:
        drawn = drawn * levels(key, extent, shards, -0.22, 0.18)
    return jnp.clip(drawn, -most, most).astype(kind)


def setup_inputs(seed: int = 0) -> dict:
    streams_of = jax.random.split(jax.random.key(seed), 8)
    matrix = noise(streams_of[0], (ROWS, P_SIZE), 1.0, 6.0, ((0, 128),))
    leaf_basis = noise(streams_of[1], (ROWS, K), LEAF_ROWS ** -0.5, 0.1875, ((0, 128),))
    leaf_tri = draw_leaf_tri(jax.random.fold_in(streams_of[7], 71), 0)
    inner_basis = draw_inner_basis(jax.random.fold_in(streams_of[7], 71), 0)
    inner_tri = draw_inner_tri(jax.random.fold_in(streams_of[7], 71), 0)
    outer_basis = draw_outer_basis(jax.random.fold_in(streams_of[7], 71), 0)
    outer_tri = draw_outer_tri(jax.random.fold_in(streams_of[7], 71), 0)
    return {"matrix": matrix, "leaf_basis": leaf_basis, "leaf_tri": leaf_tri, "inner_basis": inner_basis, "inner_tri": inner_tri, "outer_basis": outer_basis, "outer_tri": outer_tri}


def leaf_reflect(panel_rows, reflectors, triangle):
    rank_width = triangle.shape[-1]
    projected = jnp.dot(reflectors.T, panel_rows, preferred_element_type=jnp.float32)
    mixing = jnp.dot(triangle.astype(jnp.float32).T, projected, precision=lax.Precision.HIGHEST)
    return panel_rows[:rank_width].astype(jnp.float32) - jnp.dot(reflectors[:rank_width].astype(jnp.float32), mixing, precision=lax.Precision.HIGHEST)


def node_reflect(panel_rows, reflectors, triangle):
    rank_width = triangle.shape[-1]
    basis = reflectors.astype(jnp.float32)
    projected = jnp.dot(basis.T, panel_rows, precision=lax.Precision.HIGHEST)
    mixing = jnp.dot(triangle.astype(jnp.float32).T, projected, precision=lax.Precision.HIGHEST)
    return panel_rows[:rank_width] - jnp.dot(basis[:rank_width], mixing, precision=lax.Precision.HIGHEST)


def leaf_tuple(packed):
    return leaf_reflect(packed[0], packed[1], packed[2])


def node_tuple(packed):
    return node_reflect(packed[0], packed[1], packed[2])


def reference(matrix, leaf_basis, leaf_tri, inner_basis, inner_tri, outer_basis, outer_tri):
    count_leaves = N_GRP * N_LEAF
    blocks = matrix.reshape(count_leaves, LEAF_ROWS, P_SIZE)
    leaf_bases = leaf_basis.reshape(count_leaves, LEAF_ROWS, K)
    summits = lax.map(leaf_tuple, (blocks, leaf_bases, leaf_tri))
    summits = summits.reshape(N_GRP, N_LEAF, K, P_SIZE)
    for height in range(LEAF_DEPTH):
        stride = 2 ** (height + 1)
        stacked = summits.reshape(N_GRP * (summits.shape[1] // 2), 2 * K, P_SIZE)
        node_basis = inner_basis[:, ::stride, height].reshape(-1, 2 * K, K)
        node_tri = inner_tri[:, ::stride, height].reshape(-1, K, K)
        summits = lax.map(node_tuple, (stacked, node_basis, node_tri)).reshape(N_GRP, -1, K, P_SIZE)
    summits = summits.reshape(N_GRP, K, P_SIZE)
    for height in range(GRP_DEPTH):
        stride = 2 ** (height + 1)
        stacked = summits.reshape(-1, 2 * K, P_SIZE)
        node_basis = outer_basis[::stride, 0, height]
        node_tri = outer_tri[::stride, 0, height]
        summits = lax.map(node_tuple, (stacked, node_basis, node_tri))
    return summits[0].astype(jnp.bfloat16)
```

```python
import functools

import jax
import jax.numpy as jnp
from jax import lax
from jax.experimental import pallas as pl
from jax.experimental.pallas import tpu as pltpu
from jax.sharding import Mesh, PartitionSpec as P

F32 = jnp.float32
BF16 = jnp.bfloat16
NT = (((1,), (1,)), ((), ()))
NN = (((1,), (0,)), ((), ()))
VMEM = pl.BlockSpec(memory_space=pltpu.VMEM)
ANY = pl.BlockSpec(memory_space=pl.ANY)


def split_dot(rows, weights, dims):
    count = rows.shape[0]
    high = rows.astype(BF16)
    low = (rows - high.astype(F32)).astype(BF16)
    both = lax.dot_general(
        jnp.concatenate([high, low], axis=0), weights, dims, preferred_element_type=F32
    )
    return both[:count] + both[count:]


def leaf_kernel(take_other, x_ref, v_ref, f_ref, out_ref):
    half, width = out_ref.shape
    core = lax.axis_index("core")
    side = 1 - core if take_other else core
    row = lax.broadcasted_iota(jnp.int32, (half, 2 * half), 0)
    column = lax.broadcasted_iota(jnp.int32, (half, 2 * half), 1)
    wanted = (row // 4) * 8 + side * 4 + row % 4
    pick = jnp.where(column == wanted, 1.0, 0.0).astype(BF16)
    panel = lax.dot_general(pick, x_ref[...], NT, preferred_element_type=F32)
    projected = lax.dot_general(panel.astype(BF16), v_ref[...], NN, preferred_element_type=F32)
    mixing = split_dot(projected, f_ref[...], NN)
    out_ref[...] = panel[:, :width] - split_dot(mixing, v_ref[:width, :], NT)


def chain_kernel(own_ref, other_ref, ib_ref, it_ref, ob_ref, ot_ref, out_ref, v_buf, f_buf, sems):
    width = own_ref.shape[1]
    inner = ib_ref.shape[0]
    levels = v_buf.shape[0]

    def copies(level):
        basis, tri = (ib_ref, it_ref) if level < inner else (ob_ref, ot_ref)
        at = level if level < inner else level - inner
        return (
            pltpu.make_async_copy(basis.at[at], v_buf.at[level], sems.at[level, 0]),
            pltpu.make_async_copy(tri.at[at], f_buf.at[level], sems.at[level, 1]),
        )

    for level in range(levels):
        for copy in copies(level):
            copy.start()
    core = lax.axis_index("core")
    place = lax.axis_index("group") * lax.axis_size("chip") + lax.axis_index("chip")
    for level in range(levels):
        for copy in copies(level):
            copy.wait()
        if level == 0:
            own, other = own_ref[...], other_ref[...]
            base = jnp.where(core == 0, own, other)
            joined = jnp.concatenate([base, jnp.where(core == 0, other, own)], axis=1)
            projected = split_dot(joined, v_buf[level], NN)
        else:
            bit = jnp.right_shift(place, level - 1) & 1
            base = jnp.where(bit == 0, summit, 0.0)
            start = pl.multiple_of(bit * width, width)
            projected = split_dot(summit, v_buf[level, pl.ds(start, width), :], NN)
        mixing = split_dot(projected, f_buf[level], NN)
        summit = base - split_dot(mixing, v_buf[level, :width, :], NT)
    out_ref[...] = summit


def per_device(matrix, leaf_basis, leaf_tri, inner_basis, inner_tri, outer_basis, outer_tri):
    width = leaf_tri.shape[-1]
    half = matrix.shape[1] // 2
    levels = inner_basis.shape[2] + outer_basis.shape[2]

    def leaf(take_other):
        return pl.pallas_call(
            functools.partial(leaf_kernel, take_other),
            out_shape=jax.ShapeDtypeStruct((half, width), F32),
            in_specs=[VMEM] * 3,
            out_specs=VMEM,
            cost_estimate=pl.CostEstimate(
                flops=2 * 4 * width**3, bytes_accessed=4 * 2**20, transcendentals=0
            ),
            compiler_params=pltpu.CompilerParams(vmem_limit_bytes=24 * 2**20),
        )(matrix, leaf_basis, leaf_tri[0])

    sent = leaf(True)
    other = lax.ppermute(sent, "core", [(0, 1), (1, 0)])
    own = leaf(False)
    terms = pl.pallas_call(
        chain_kernel,
        out_shape=jax.ShapeDtypeStruct((half, width), F32),
        in_specs=[VMEM, VMEM, ANY, ANY, ANY, ANY],
        out_specs=VMEM,
        scratch_shapes=[
            pltpu.VMEM((levels, 2 * width, width), BF16),
            pltpu.VMEM((levels, width, width), BF16),
            pltpu.SemaphoreType.DMA((levels, 2)),
        ],
        cost_estimate=pl.CostEstimate(
            flops=2 * 22 * width**3, bytes_accessed=12 * 2**20, transcendentals=0
        ),
        compiler_params=pltpu.CompilerParams(vmem_limit_bytes=40 * 2**20),
    )(own, other, inner_basis[0, 0], inner_tri[0, 0], outer_basis[0, 0], outer_tri[0, 0])
    chips = lax.axis_size("group") * lax.axis_size("chip")
    blocks = terms.reshape(chips, half // chips, width)
    swapped = lax.all_to_all(blocks, ("group", "chip"), 0, 0, tiled=True)
    return jnp.sum(swapped, axis=0).T.astype(BF16)


def solution(mesh):
    groups, leaves = mesh.devices.shape
    fine = Mesh(mesh.devices.reshape(groups, leaves // 2, 2), ("group", "chip", "core"))
    every = ("group", "chip", "core")
    leaf = ("chip", "core")
    placed = (
        P(every, None),
        P(every, None),
        P(every, None, None),
        P("group", leaf, None, None, None),
        P("group", leaf, None, None, None),
        P("group", leaf, None, None, None),
        P("group", leaf, None, None, None),
    )
    return jax.shard_map(
        per_device, mesh=fine, in_specs=placed, out_specs=P(None, every), check_vma=False
    )
```

```python
import functools

import jax
import jax.numpy as jnp
from jax import lax
from jax.experimental import pallas as pl
from jax.experimental.pallas import tpu as pltpu
from jax.sharding import Mesh, PartitionSpec as P

PIECES = 1
F32 = jnp.float32
BF16 = jnp.bfloat16
NT = (((1,), (1,)), ((), ()))
NN = (((1,), (0,)), ((), ()))
VMEM = pl.BlockSpec(memory_space=pltpu.VMEM)
HBM = pl.BlockSpec(memory_space=pltpu.HBM)


def split_dot(rows, weights, dims):
    count = rows.shape[0]
    high = rows.astype(BF16)
    low = (rows - high.astype(F32)).astype(BF16)
    both = lax.dot_general(
        jnp.concatenate([high, low], axis=0), weights, dims, preferred_element_type=F32
    )
    return both[:count] + both[count:]


def pick_rows(side, half):
    row = lax.broadcasted_iota(jnp.int32, (half, 2 * half), 0)
    column = lax.broadcasted_iota(jnp.int32, (half, 2 * half), 1)
    wanted = (row // 4) * 8 + side * 4 + row % 4
    return jnp.where(column == wanted, 1.0, 0.0).astype(BF16)


def mix_dot(rows, triangle):
    half = triangle.shape[0] // 2
    left = split_dot(rows[:, :half], triangle[:half, :half], NN)
    right = split_dot(rows, triangle[:, half:], NN)
    return jnp.concatenate([left, right], axis=1)


def fetch(sources, targets, sems):
    copies = [
        pltpu.make_async_copy(source, target, sems.at[index])
        for index, (source, target) in enumerate(zip(sources, targets, strict=True))
    ]
    for copy in copies:
        copy.start()
    return copies


def finish_leaf(top, projected, v_ref, f_ref):
    mixing = mix_dot(projected, f_ref[...])
    return top - split_dot(mixing, v_ref[: f_ref.shape[0], :], NT)


def send_kernel(x_hbm, v_hbm, f_hbm, ib_hbm, it_hbm, out_ref, x_ref, v_ref, f_ref, wv_ref, wf_ref, sems):
    rows = x_hbm.shape[0]
    size = rows // PIECES
    spans = [pl.ds(piece * size, size) for piece in range(PIECES)]
    sources = [ref.at[span] for ref in (x_hbm, v_hbm) for span in spans]
    targets = [ref.at[span] for ref in (x_ref, v_ref) for span in spans]
    sources.append(f_hbm)
    targets.append(f_ref)
    for level in range(wv_ref.shape[0]):
        sources += [ib_hbm.at[level], it_hbm.at[level]]
        targets += [wv_ref.at[level], wf_ref.at[level]]
    copies = fetch(sources, targets, sems)
    pick = pick_rows(1 - lax.axis_index("core"), out_ref.shape[0])
    for copy in copies[:PIECES]:
        copy.wait()
    panel = lax.dot_general(pick, x_ref[...], NT, preferred_element_type=F32)
    for copy in copies[PIECES : 2 * PIECES + 1]:
        copy.wait()
    projected = lax.dot_general(panel.astype(BF16), v_ref[...], NN, preferred_element_type=F32)
    out_ref[...] = finish_leaf(panel[:, : f_ref.shape[0]], projected, v_ref, f_ref)
    for copy in copies[2 * PIECES + 1 :]:
        copy.wait()


def keep_kernel(x_ref, v_ref, f_ref, out_ref):
    pick = pick_rows(lax.axis_index("core"), out_ref.shape[0])
    panel = lax.dot_general(pick, x_ref[...], NT, preferred_element_type=F32)
    projected = lax.dot_general(panel.astype(BF16), v_ref[...], NN, preferred_element_type=F32)
    out_ref[...] = finish_leaf(panel[:, : f_ref.shape[0]], projected, v_ref, f_ref)


def chain_kernel(
    own_ref, other_ref, wv_ref, wf_ref, ib_hbm, it_hbm, ob_hbm, ot_hbm, out_ref, v_buf, f_buf, sems
):
    width = own_ref.shape[1]
    early, inner, outer = wv_ref.shape[0], ib_hbm.shape[0], ob_hbm.shape[0]
    sources = []
    for level in range(early, inner):
        sources += [ib_hbm.at[level], it_hbm.at[level]]
    for level in range(outer):
        sources += [ob_hbm.at[level], ot_hbm.at[level]]
    late = inner + outer - early
    targets = [buf.at[index] for index in range(late) for buf in (v_buf, f_buf)]
    copies = fetch(sources, targets, sems)
    levels = [(wv_ref, wf_ref, at, []) for at in range(early)]
    levels += [(v_buf, f_buf, at, copies[2 * at : 2 * at + 2]) for at in range(late)]
    core = lax.axis_index("core")
    place = lax.axis_index("group") * lax.axis_size("chip") + lax.axis_index("chip")
    for level, (basis, tri, at, waits) in enumerate(levels):
        for copy in waits:
            copy.wait()
        if level == 0:
            own, other = own_ref[...], other_ref[...]
            base = jnp.where(core == 0, own, other)
            joined = jnp.concatenate([base, jnp.where(core == 0, other, own)], axis=1)
            projected = split_dot(joined, basis[at], NN)
        else:
            bit = jnp.right_shift(place, level - 1) & 1
            base = jnp.where(bit == 0, summit, 0.0)
            start = pl.multiple_of(bit * width, width)
            projected = split_dot(summit, basis[at, pl.ds(start, width), :], NN)
        mixing = mix_dot(projected, tri[at])
        summit = base - split_dot(mixing, basis[at, :width, :], NT)
    out_ref[...] = summit


def in_hbm(array):
    return pltpu.with_memory_space_constraint(array, pltpu.HBM)


def estimate(units, mebibytes):
    return pl.CostEstimate(
        flops=units * 2 * 512**3, bytes_accessed=mebibytes * 2**20, transcendentals=0
    )


def per_device(matrix, leaf_basis, leaf_tri, inner_basis, inner_tri, outer_basis, outer_tri):
    rows, width = leaf_basis.shape
    half = matrix.shape[1] // 2
    inner, outer = inner_basis.shape[2], outer_basis.shape[2]
    ahead = 2
    trees = (in_hbm(inner_basis[0, 0]), in_hbm(inner_tri[0, 0]))

    def basis_of(levels):
        return jax.ShapeDtypeStruct((levels, rows, width), BF16)

    def tri_of(levels):
        return jax.ShapeDtypeStruct((levels, width, width), BF16)

    summit = jax.ShapeDtypeStruct((half, width), F32)
    sent, x, v, f, wv, wf = pl.pallas_call(
        send_kernel,
        out_shape=(
            summit,
            jax.ShapeDtypeStruct(matrix.shape, BF16),
            jax.ShapeDtypeStruct((rows, width), BF16),
            jax.ShapeDtypeStruct((width, width), BF16),
            basis_of(ahead),
            tri_of(ahead),
        ),
        in_specs=[HBM] * 5,
        out_specs=(VMEM,) * 6,
        scratch_shapes=[pltpu.SemaphoreType.DMA((2 * PIECES + 1 + 2 * ahead,))],
        cost_estimate=estimate(4, 4),
        compiler_params=pltpu.CompilerParams(vmem_limit_bytes=16 * 2**20),
    )(in_hbm(matrix), in_hbm(leaf_basis), in_hbm(leaf_tri[0]), *trees)
    other = lax.ppermute(sent, "core", [(0, 1), (1, 0)])
    own = pl.pallas_call(
        keep_kernel,
        out_shape=summit,
        in_specs=[VMEM] * 3,
        out_specs=VMEM,
        cost_estimate=estimate(4, 4),
        compiler_params=pltpu.CompilerParams(vmem_limit_bytes=16 * 2**20),
    )(x, v, f)
    late = inner + outer - ahead
    terms = pl.pallas_call(
        chain_kernel,
        out_shape=summit,
        in_specs=[VMEM] * 4 + [HBM] * 4,
        out_specs=VMEM,
        scratch_shapes=[
            pltpu.VMEM((late, rows, width), BF16),
            pltpu.VMEM((late, width, width), BF16),
            pltpu.SemaphoreType.DMA((2 * late,)),
        ],
        cost_estimate=estimate(22, 12),
        compiler_params=pltpu.CompilerParams(vmem_limit_bytes=24 * 2**20),
    )(own, other, wv, wf, *trees, in_hbm(outer_basis[0, 0]), in_hbm(outer_tri[0, 0]))
    chips = lax.axis_size("group") * lax.axis_size("chip")
    blocks = terms.reshape(chips, half // chips, width)
    swapped = lax.all_to_all(blocks, ("group", "chip"), 0, 0, tiled=True)
    return jnp.sum(swapped, axis=0).T.astype(BF16)


def solution(mesh):
    groups, leaves = mesh.devices.shape
    fine = Mesh(mesh.devices.reshape(groups, leaves // 2, 2), ("group", "chip", "core"))
    every = ("group", "chip", "core")
    leaf = ("chip", "core")
    placed = (
        P(every, None),
        P(every, None),
        P(every, None, None),
        P("group", leaf, None, None, None),
        P("group", leaf, None, None, None),
        P("group", leaf, None, None, None),
        P("group", leaf, None, None, None),
    )
    return jax.shard_map(
        per_device, mesh=fine, in_specs=placed, out_specs=P(None, every), check_vma=False
    )
```

```python
import functools

import jax
import jax.numpy as jnp
from jax import lax
from jax.experimental import pallas as pl
from jax.experimental.pallas import tpu as pltpu
from jax.sharding import Mesh, PartitionSpec as P

NT = (((1,), (1,)), ((), ()))
NN = (((1,), (0,)), ((), ()))
TILE = 256
UNITS = 2
GROUPS = 4
F32 = jnp.float32
BF16 = jnp.bfloat16
VMEM = pl.BlockSpec(memory_space=pltpu.VMEM)
HBM = pl.BlockSpec(memory_space=pltpu.HBM)


def pair(rows):
    high = rows.astype(BF16)
    return high, (rows - high.astype(F32)).astype(BF16)


def pick_rows(side, half):
    row = lax.broadcasted_iota(jnp.int32, (half, 2 * half), 0)
    column = lax.broadcasted_iota(jnp.int32, (half, 2 * half), 1)
    wanted = (row // 4) * 8 + side * 4 + row % 4
    return jnp.where(column == wanted, 1.0, 0.0).astype(BF16)


def tile(index):
    return slice(index * TILE, (index + 1) * TILE)


def by_columns(depth):
    return lambda unit: range(depth)


def triangle_plan(unit):
    return range(unit + 1)


def run_stages(stages, lhs, sums):
    groups = len(lhs)
    slots = []
    for index, (plan, _, _) in enumerate(stages):
        rounds = max(len(plan(unit)) for unit in range(UNITS))
        slots += [(index, group, at) for group in range(groups) for at in range(rounds)]

    def depth_of(unit, slot):
        index, group, at = slot
        order = list(stages[index][0](unit))
        order = order[::-1] if group % 2 else order
        return order[at] if at < len(order) else None

    loads = [[] for _ in range(UNITS)]
    load_at = [{} for _ in range(UNITS)]
    for unit in range(UNITS):
        held = None
        for position, slot in enumerate(slots):
            depth = depth_of(unit, slot)
            if depth is not None and (slot[0], depth) != held:
                held = (slot[0], depth)
                load_at[unit][position] = len(loads[unit])
                loads[unit].append(held)
    pushed = [0] * UNITS

    def push(unit, count):
        while pushed[unit] < min(count, len(loads[unit])):
            index, depth = loads[unit][pushed[unit]]
            matrix, transpose = stages[index][1](unit, depth)
            pltpu.matmul_push_rhs(matrix, pushed[unit] % 2, unit, transpose=transpose)
            pushed[unit] += 1

    rows = {(0, group): lhs[group] for group in range(groups)}
    waiting = [(index, group) for index in range(len(stages)) for group in range(groups)]

    def finish():
        index, group = waiting.pop(0)
        tiles = [pltpu.matmul_pop(sums[unit][group]) for unit in range(UNITS)]
        rows[index + 1, group] = stages[index][2](group, tiles)

    for position, slot in enumerate(slots):
        while slot[:2] not in rows:
            finish()
        for part in range(len(rows[slot[:2]][0])):
            for unit in range(UNITS):
                depth = depth_of(unit, slot)
                if depth is None:
                    continue
                load = load_at[unit].get(position) if part == 0 else None
                if load is not None:
                    push(unit, load + 1)
                pltpu.matmul_acc_lhs(
                    sums[unit][slot[1]],
                    rows[slot[:2]][depth][part],
                    load_staged_rhs=None if load is None else load % 2,
                )
                if load is not None:
                    push(unit, load + 2)
    while waiting:
        finish()


def with_sums(body, rows):
    def scoped(*flat):
        body([flat[unit * GROUPS : (unit + 1) * GROUPS] for unit in range(UNITS)])

    pl.run_scoped(
        scoped,
        *[
            pltpu.ACC(unit)((rows // GROUPS, TILE), F32)
            for unit in range(UNITS)
            for _ in range(GROUPS)
        ],
    )


def pairs(group, tiles):
    return [pair(values) for values in tiles]


def once(copies):
    done = set()

    def ready(index=0):
        if index not in done:
            done.add(index)
            copies[index].wait()

    return ready


def fetch(sources, targets, sems):
    copies = [
        pltpu.make_async_copy(source, target, sems.at[index])
        for index, (source, target) in enumerate(zip(sources, targets, strict=True))
    ]
    for copy in copies:
        copy.start()
    return copies


def split_dot(rows, weights, dims):
    count = rows.shape[0]
    high = rows.astype(BF16)
    low = (rows - high.astype(F32)).astype(BF16)
    both = lax.dot_general(
        jnp.concatenate([high, low], axis=0), weights, dims, preferred_element_type=F32
    )
    return both[:count] + both[count:]


def mix_dot(rows, triangle):
    half = triangle.shape[0] // 2
    left = split_dot(rows[:, :half], triangle[:half, :half], NN)
    right = split_dot(rows, triangle[:, half:], NN)
    return jnp.concatenate([left, right], axis=1)


def finish_leaf(top, projected, v_ref, f_ref):
    mixing = mix_dot(projected, f_ref[...])
    return top - split_dot(mixing, v_ref[: f_ref.shape[0], :], NT)


def send_kernel(x_hbm, v_hbm, f_hbm, ib_hbm, it_hbm, out_ref, x_ref, v_ref, f_ref, wv_ref, wf_ref, sems):
    sources, targets = [x_hbm, v_hbm, f_hbm], [x_ref, v_ref, f_ref]
    for level in range(wv_ref.shape[0]):
        sources += [ib_hbm.at[level], it_hbm.at[level]]
        targets += [wv_ref.at[level], wf_ref.at[level]]
    copies = fetch(sources, targets, sems)
    pick = pick_rows(1 - lax.axis_index("core"), out_ref.shape[0])
    copies[0].wait()
    panel = lax.dot_general(pick, x_ref[...], NT, preferred_element_type=F32)
    copies[1].wait()
    copies[2].wait()
    projected = lax.dot_general(panel.astype(BF16), v_ref[...], NN, preferred_element_type=F32)
    out_ref[...] = finish_leaf(panel[:, : f_ref.shape[0]], projected, v_ref, f_ref)
    for copy in copies[3:]:
        copy.wait()


def keep_kernel(x_ref, v_ref, f_ref, out_ref):
    pick = pick_rows(lax.axis_index("core"), out_ref.shape[0])
    panel = lax.dot_general(pick, x_ref[...], NT, preferred_element_type=F32)
    projected = lax.dot_general(panel.astype(BF16), v_ref[...], NN, preferred_element_type=F32)
    out_ref[...] = finish_leaf(panel[:, : f_ref.shape[0]], projected, v_ref, f_ref)


def chain_kernel(
    own_ref, other_ref, wv_ref, wf_ref, ib_hbm, it_hbm, ob_hbm, ot_hbm, out_ref, v_buf, f_buf, sems
):
    rows, width = own_ref.shape
    count = rows // GROUPS
    early, inner, outer = wv_ref.shape[0], ib_hbm.shape[0], ob_hbm.shape[0]
    sources = []
    for level in range(early, inner):
        sources += [ib_hbm.at[level], it_hbm.at[level]]
    for level in range(outer):
        sources += [ob_hbm.at[level], ot_hbm.at[level]]
    late = inner + outer - early
    targets = [buf.at[index] for index in range(late) for buf in (v_buf, f_buf)]
    arrived = once(fetch(sources, targets, sems))
    core = lax.axis_index("core")
    place = lax.axis_index("group") * lax.axis_size("chip") + lax.axis_index("chip")
    summit = [None] * GROUPS

    def level_stages(level):
        basis_ref, tri_ref, at = (
            (wv_ref, wf_ref, level) if level < early else (v_buf, f_buf, level - early)
        )
        bit = jnp.right_shift(place, level - 1) & 1 if level else 0
        first = bit * width

        def basis(out, depth):
            if level >= early:
                arrived(2 * at)
            start = pl.multiple_of(first + depth * TILE, TILE)
            return basis_ref[at, pl.ds(start, TILE), tile(out)], False

        def triangle(out, depth):
            if level >= early:
                arrived(2 * at + 1)
            return tri_ref[at, tile(depth), tile(out)], False

        def top(out, depth):
            return basis_ref[at, tile(out), tile(depth)], True

        def after(group, tiles):
            base = summit[group]
            if level:
                base = [jnp.where(bit == 0, values, 0.0) for values in base]
            summit[group] = [kept - values for kept, values in zip(base, tiles, strict=True)]
            return pairs(group, summit[group])

        def last(group, tiles):
            after(group, tiles)
            left, right = summit[group]
            upper = lax.broadcasted_iota(jnp.int32, (count, TILE), 0) % 8 < 4
            even = jnp.where(upper, left, pltpu.roll(right, 4, 0))
            odd = jnp.where(upper, pltpu.roll(left, count - 4, 0), right)
            for index, values in enumerate((even, odd)):
                at = pl.ds(group * count // 8, count // 8)
                out_ref[at, index] = values.reshape(count // 8, 8, TILE)

        end = last if level == inner + outer - 1 else after
        return [
            (by_columns(2 if level else 4), basis, pairs),
            (triangle_plan, triangle, pairs),
            (by_columns(2), top, end),
        ]

    lhs = []
    for group in range(GROUPS):
        at = pl.ds(group * count, count)
        own = [own_ref[at, tile(out)] for out in range(2)]
        other = [other_ref[at, tile(out)] for out in range(2)]
        summit[group] = [jnp.where(core == 0, a, b) for a, b in zip(own, other, strict=True)]
        upper = [jnp.where(core == 0, b, a) for a, b in zip(own, other, strict=True)]
        lhs.append(pairs(group, summit[group] + upper))
    stages = [stage for level in range(inner + outer) for stage in level_stages(level)]
    with_sums(lambda sums: run_stages(stages, lhs, sums), rows)


def in_hbm(array):
    return pltpu.with_memory_space_constraint(array, pltpu.HBM)


def sum_kernel(terms_ref, out_ref):
    total = jnp.sum(terms_ref[...], axis=0)
    out_ref[...] = jnp.concatenate([total[:4], total[4:]], axis=1).astype(BF16)


def estimate(units, mebibytes):
    return pl.CostEstimate(
        flops=units * 2 * 512**3, bytes_accessed=mebibytes * 2**20, transcendentals=0
    )


def per_device(matrix, leaf_basis, leaf_tri, inner_basis, inner_tri, outer_basis, outer_tri):
    rows, width = leaf_basis.shape
    half = matrix.shape[1] // 2
    inner, outer = inner_basis.shape[2], outer_basis.shape[2]
    ahead = 2
    trees = (in_hbm(inner_basis[0, 0]), in_hbm(inner_tri[0, 0]))

    def basis_of(levels):
        return jax.ShapeDtypeStruct((levels, rows, width), BF16)

    def tri_of(levels):
        return jax.ShapeDtypeStruct((levels, width, width), BF16)

    summit = jax.ShapeDtypeStruct((half, width), F32)
    sent, x, v, f, wv, wf = pl.pallas_call(
        send_kernel,
        out_shape=(
            summit,
            jax.ShapeDtypeStruct(matrix.shape, BF16),
            jax.ShapeDtypeStruct((rows, width), BF16),
            jax.ShapeDtypeStruct((width, width), BF16),
            basis_of(ahead),
            tri_of(ahead),
        ),
        in_specs=[HBM] * 5,
        out_specs=(VMEM,) * 6,
        scratch_shapes=[pltpu.SemaphoreType.DMA((3 + 2 * ahead,))],
        cost_estimate=estimate(4, 4),
        compiler_params=pltpu.CompilerParams(vmem_limit_bytes=16 * 2**20),
    )(in_hbm(matrix), in_hbm(leaf_basis), in_hbm(leaf_tri[0]), *trees)
    other = lax.ppermute(sent, "core", [(0, 1), (1, 0)])
    own = pl.pallas_call(
        keep_kernel,
        out_shape=summit,
        in_specs=[VMEM] * 3,
        out_specs=VMEM,
        cost_estimate=estimate(4, 4),
        compiler_params=pltpu.CompilerParams(vmem_limit_bytes=16 * 2**20),
    )(x, v, f)
    late = inner + outer - ahead
    terms = pl.pallas_call(
        chain_kernel,
        out_shape=jax.ShapeDtypeStruct((half // 8, 2, 8, TILE), F32),
        in_specs=[VMEM] * 4 + [HBM] * 4,
        out_specs=VMEM,
        scratch_shapes=[
            pltpu.VMEM((late, rows, width), BF16),
            pltpu.VMEM((late, width, width), BF16),
            pltpu.SemaphoreType.DMA((2 * late,)),
        ],
        cost_estimate=estimate(22, 12),
        compiler_params=pltpu.CompilerParams(vmem_limit_bytes=24 * 2**20),
    )(own, other, wv, wf, *trees, in_hbm(outer_basis[0, 0]), in_hbm(outer_tri[0, 0]))
    chips = lax.axis_size("group") * lax.axis_size("chip")
    blocks = terms.reshape(chips, 8, TILE)
    swapped = lax.all_to_all(blocks, ("group", "chip"), 0, 0, tiled=True)
    columns = pl.pallas_call(
        sum_kernel,
        out_shape=jax.ShapeDtypeStruct((half // chips, width), BF16),
        in_specs=[VMEM],
        out_specs=VMEM,
        compiler_params=pltpu.CompilerParams(vmem_limit_bytes=8 * 2**20),
    )(swapped)
    return columns.T


def solution(mesh):
    groups, leaves = mesh.devices.shape
    fine = Mesh(mesh.devices.reshape(groups, leaves // 2, 2), ("group", "chip", "core"))
    every = ("group", "chip", "core")
    leaf = ("chip", "core")
    placed = (
        P(every, None),
        P(every, None),
        P(every, None, None),
        P("group", leaf, None, None, None),
        P("group", leaf, None, None, None),
        P("group", leaf, None, None, None),
        P("group", leaf, None, None, None),
    )
    return jax.shard_map(
        per_device, mesh=fine, in_specs=placed, out_specs=P(None, every), check_vma=False
    )
```

```python
import functools

import jax
import jax.numpy as jnp
from jax import lax
from jax.experimental import pallas as pl
from jax.experimental.pallas import tpu as pltpu
from jax.sharding import Mesh, PartitionSpec as P

TILE = 256
UNITS = 2
GROUPS = (96, 80, 80)
F32 = jnp.float32
BF16 = jnp.bfloat16
VMEM = pl.BlockSpec(memory_space=pltpu.VMEM)
HBM = pl.BlockSpec(memory_space=pltpu.HBM)


def pair(rows):
    high = rows.astype(BF16)
    return high, (rows - high.astype(F32)).astype(BF16)


def pick_rows(side, half):
    row = lax.broadcasted_iota(jnp.int32, (half, 2 * half), 0)
    column = lax.broadcasted_iota(jnp.int32, (half, 2 * half), 1)
    wanted = (row // 4) * 8 + side * 4 + row % 4
    return jnp.where(column == wanted, 1.0, 0.0).astype(BF16)


def tile(index):
    return slice(index * TILE, (index + 1) * TILE)


def by_columns(depth):
    return lambda unit: range(depth)


def triangle_plan(unit):
    return range(unit + 1)


def run_stages(stages, lhs, sums):
    groups = len(GROUPS)
    slots = []
    for index, (plan, _, _) in enumerate(stages):
        rounds = max(len(plan(unit)) for unit in range(UNITS))
        slots += [(index, group, at) for group in range(groups) for at in range(rounds)]

    def depth_of(unit, slot):
        index, group, at = slot
        order = list(stages[index][0](unit))
        order = order[::-1] if group % 2 else order
        return order[at] if at < len(order) else None

    loads = [[] for _ in range(UNITS)]
    load_at = [{} for _ in range(UNITS)]
    for unit in range(UNITS):
        held = None
        for position, slot in enumerate(slots):
            depth = depth_of(unit, slot)
            if depth is not None and (slot[0], depth) != held:
                held = (slot[0], depth)
                load_at[unit][position] = len(loads[unit])
                loads[unit].append(held)
    pushed = [0] * UNITS

    def push(unit, count):
        while pushed[unit] < min(count, len(loads[unit])):
            index, depth = loads[unit][pushed[unit]]
            matrix, transpose = stages[index][1](unit, depth)
            pltpu.matmul_push_rhs(matrix, pushed[unit] % 2, unit, transpose=transpose)
            pushed[unit] += 1

    rows = {}
    waiting = [(index, group) for index in range(len(stages)) for group in range(groups)]

    def finish():
        index, group = waiting.pop(0)
        tiles = [pltpu.matmul_pop(sums[unit][group]) for unit in range(UNITS)]
        rows[index + 1, group] = stages[index][2](group, tiles)

    for position, slot in enumerate(slots):
        while slot[:2] not in rows:
            if slot[0]:
                finish()
            else:
                rows[slot[:2]] = lhs(slot[1])
        for part in range(len(rows[slot[:2]][0])):
            for unit in range(UNITS):
                depth = depth_of(unit, slot)
                if depth is None:
                    continue
                load = load_at[unit].get(position) if part == 0 else None
                if load is not None:
                    push(unit, load + 1)
                pltpu.matmul_acc_lhs(
                    sums[unit][slot[1]],
                    rows[slot[:2]][depth][part],
                    load_staged_rhs=None if load is None else load % 2,
                )
                if load is not None:
                    push(unit, load + 2)
    while waiting:
        finish()


def with_sums(body, kinds=1):
    def scoped(*flat):
        flat = iter(flat)
        body(*[[[next(flat) for _ in GROUPS] for _ in range(UNITS)] for _ in range(kinds)])

    pl.run_scoped(
        scoped,
        *[
            pltpu.ACC(unit)((count, TILE), F32)
            for _ in range(kinds)
            for unit in range(UNITS)
            for count in GROUPS
        ],
    )


def pairs(group, tiles):
    return [pair(values) for values in tiles]


def once(copies):
    done = set()

    def ready(index):
        if index not in done:
            done.add(index)
            copies[index].wait()

    return ready


def fetch(sources, targets, sems):
    copies = [
        pltpu.make_async_copy(source, target, sems.at[index])
        for index, (source, target) in enumerate(zip(sources, targets, strict=True))
    ]
    for copy in copies:
        copy.start()
    return copies


def run_leaf(side, x_ref, v_ref, f_ref, out_ref, ready):
    blocks = x_ref.shape[0] // TILE
    offsets = [sum(GROUPS[:group]) for group in range(len(GROUPS))]
    spans = [slice(start, start + count) for start, count in zip(offsets, GROUPS, strict=True)]
    pick = pick_rows(side, out_ref.shape[0])

    def body(first, second, sums, late):
        pushed = [0] * UNITS

        def push(unit, count):
            while pushed[unit] < min(count, 2 * blocks):
                load = pushed[unit]
                if load < blocks:
                    out, depth = UNITS * (load // 2) + unit, load % 2
                    ready(out)
                    matrix = x_ref[tile(out), tile(depth)]
                else:
                    ready(load)
                    matrix = v_ref[tile(load - blocks), tile(unit)]
                pltpu.matmul_push_rhs(matrix, load % 2, unit, transpose=load < blocks)
                pushed[unit] += 1

        def product(load, totals, rows):
            for unit in range(UNITS):
                push(unit, load + 1)
                for group, part in enumerate(rows):
                    pltpu.matmul_acc_lhs(
                        totals[unit][group], part, load_staged_rhs=None if group else load % 2
                    )
                push(unit, load + 2)

        for load in range(blocks):
            totals = first if load < 2 else second
            product(load, totals, [pick[span, tile(load % 2)] for span in spans])
        tops = []
        for index, totals in enumerate((first, second)):
            panel = [
                [pltpu.matmul_pop(totals[unit][group]) for group in range(len(GROUPS))]
                for unit in range(UNITS)
            ]
            if index == 0:
                tops = panel
            for unit in range(UNITS):
                rows = [values.astype(BF16) for values in panel[unit]]
                product(blocks + UNITS * index + unit, sums, rows)

        def projected(group):
            return pairs(group, [pltpu.matmul_pop(sums[unit][group]) for unit in range(UNITS)])

        def triangle(out, depth):
            ready(2 * blocks)
            return f_ref[tile(depth), tile(out)], False

        def top(out, depth):
            return v_ref[tile(out), tile(depth)], True

        def finish(group, tiles):
            for out, values in enumerate(tiles):
                out_ref[pl.ds(offsets[group], GROUPS[group]), tile(out)] = tops[out][group] - values

        run_stages(
            [(triangle_plan, triangle, pairs), (by_columns(2), top, finish)], projected, late
        )

    with_sums(body, 4)


def send_kernel(x_hbm, v_hbm, f_hbm, ib_hbm, it_hbm, out_ref, x_ref, v_ref, f_ref, wv_ref, wf_ref, sems):
    tiles = [pl.ds(block * TILE, TILE) for block in range(x_hbm.shape[0] // TILE)]
    sources = [ref.at[span] for ref in (x_hbm, v_hbm) for span in tiles] + [f_hbm]
    targets = [ref.at[span] for ref in (x_ref, v_ref) for span in tiles] + [f_ref]
    for level in range(wv_ref.shape[0]):
        sources += [ib_hbm.at[level], it_hbm.at[level]]
        targets += [wv_ref.at[level], wf_ref.at[level]]
    copies = fetch(sources, targets, sems)
    side = 1 - lax.axis_index("core")
    run_leaf(side, x_ref, v_ref, f_ref, out_ref, once(copies))
    for copy in copies[2 * len(tiles) + 1 :]:
        copy.wait()


def keep_kernel(x_ref, v_ref, f_ref, out_ref):
    run_leaf(lax.axis_index("core"), x_ref, v_ref, f_ref, out_ref, lambda index: None)


def chain_kernel(
    own_ref, other_ref, wv_ref, wf_ref, ib_hbm, it_hbm, ob_hbm, ot_hbm, out_ref, v_buf, f_buf, sems
):
    width = own_ref.shape[1]
    offsets = [sum(GROUPS[:group]) for group in range(len(GROUPS))]
    early, inner, outer = wv_ref.shape[0], ib_hbm.shape[0], ob_hbm.shape[0]
    sources = []
    for level in range(early, inner):
        sources += [ib_hbm.at[level], it_hbm.at[level]]
    for level in range(outer):
        sources += [ob_hbm.at[level], ot_hbm.at[level]]
    late = inner + outer - early
    targets = [buf.at[index] for index in range(late) for buf in (v_buf, f_buf)]
    arrived = once(fetch(sources, targets, sems))
    core = lax.axis_index("core")
    place = lax.axis_index("group") * lax.axis_size("chip") + lax.axis_index("chip")
    summit = [None] * len(GROUPS)

    def level_stages(level):
        basis_ref, tri_ref, at = (
            (wv_ref, wf_ref, level) if level < early else (v_buf, f_buf, level - early)
        )
        bit = jnp.right_shift(place, level - 1) & 1 if level else 0
        first = bit * width

        def basis(out, depth):
            if level >= early:
                arrived(2 * at)
            start = pl.multiple_of(first + depth * TILE, TILE)
            return basis_ref[at, pl.ds(start, TILE), tile(out)], False

        def triangle(out, depth):
            if level >= early:
                arrived(2 * at + 1)
            return tri_ref[at, tile(depth), tile(out)], False

        def top(out, depth):
            return basis_ref[at, tile(out), tile(depth)], True

        def after(group, tiles):
            base = summit[group]
            if level:
                base = [jnp.where(bit == 0, values, 0.0) for values in base]
            summit[group] = [kept - values for kept, values in zip(base, tiles, strict=True)]
            return pairs(group, summit[group])

        def last(group, tiles):
            after(group, tiles)
            left, right = summit[group]
            count = GROUPS[group]
            upper = lax.broadcasted_iota(jnp.int32, (count, TILE), 0) % 8 < 4
            even = jnp.where(upper, left, pltpu.roll(right, 4, 0))
            odd = jnp.where(upper, pltpu.roll(left, count - 4, 0), right)
            for index, values in enumerate((even, odd)):
                at = pl.ds(offsets[group] // 8, count // 8)
                out_ref[at, index] = values.reshape(count // 8, 8, TILE)

        end = last if level == inner + outer - 1 else after
        return [
            (by_columns(2 if level else 4), basis, pairs),
            (triangle_plan, triangle, pairs),
            (by_columns(2), top, end),
        ]

    def lhs(group):
        at = pl.ds(offsets[group], GROUPS[group])
        own = [own_ref[at, tile(out)] for out in range(2)]
        other = [other_ref[at, tile(out)] for out in range(2)]
        summit[group] = [jnp.where(core == 0, a, b) for a, b in zip(own, other, strict=True)]
        upper = [jnp.where(core == 0, b, a) for a, b in zip(own, other, strict=True)]
        return pairs(group, summit[group] + upper)

    stages = [stage for level in range(inner + outer) for stage in level_stages(level)]
    with_sums(lambda sums: run_stages(stages, lhs, sums))


def in_hbm(array):
    return pltpu.with_memory_space_constraint(array, pltpu.HBM)


def sum_kernel(terms_ref, out_ref):
    total = jnp.sum(terms_ref[...], axis=0)
    out_ref[...] = jnp.concatenate([total[:4], total[4:]], axis=1).astype(BF16)


def estimate(units, mebibytes):
    return pl.CostEstimate(
        flops=units * 2 * 512**3, bytes_accessed=mebibytes * 2**20, transcendentals=0
    )


def per_device(matrix, leaf_basis, leaf_tri, inner_basis, inner_tri, outer_basis, outer_tri):
    rows, width = leaf_basis.shape
    half = matrix.shape[1] // 2
    inner, outer = inner_basis.shape[2], outer_basis.shape[2]
    ahead = 2
    trees = (in_hbm(inner_basis[0, 0]), in_hbm(inner_tri[0, 0]))

    def basis_of(levels):
        return jax.ShapeDtypeStruct((levels, rows, width), BF16)

    def tri_of(levels):
        return jax.ShapeDtypeStruct((levels, width, width), BF16)

    summit = jax.ShapeDtypeStruct((half, width), F32)
    sent, x, v, f, wv, wf = pl.pallas_call(
        send_kernel,
        out_shape=(
            summit,
            jax.ShapeDtypeStruct(matrix.shape, BF16),
            jax.ShapeDtypeStruct((rows, width), BF16),
            jax.ShapeDtypeStruct((width, width), BF16),
            basis_of(ahead),
            tri_of(ahead),
        ),
        in_specs=[HBM] * 5,
        out_specs=(VMEM,) * 6,
        scratch_shapes=[pltpu.SemaphoreType.DMA((2 * rows // TILE + 1 + 2 * ahead,))],
        cost_estimate=estimate(4, 4),
        compiler_params=pltpu.CompilerParams(vmem_limit_bytes=16 * 2**20),
    )(in_hbm(matrix), in_hbm(leaf_basis), in_hbm(leaf_tri[0]), *trees)
    other = lax.ppermute(sent, "core", [(0, 1), (1, 0)])
    own = pl.pallas_call(
        keep_kernel,
        out_shape=summit,
        in_specs=[VMEM] * 3,
        out_specs=VMEM,
        cost_estimate=estimate(4, 4),
        compiler_params=pltpu.CompilerParams(vmem_limit_bytes=16 * 2**20),
    )(x, v, f)
    late = inner + outer - ahead
    terms = pl.pallas_call(
        chain_kernel,
        out_shape=jax.ShapeDtypeStruct((half // 8, 2, 8, TILE), F32),
        in_specs=[VMEM] * 4 + [HBM] * 4,
        out_specs=VMEM,
        scratch_shapes=[
            pltpu.VMEM((late, rows, width), BF16),
            pltpu.VMEM((late, width, width), BF16),
            pltpu.SemaphoreType.DMA((2 * late,)),
        ],
        cost_estimate=estimate(22, 12),
        compiler_params=pltpu.CompilerParams(vmem_limit_bytes=24 * 2**20),
    )(own, other, wv, wf, *trees, in_hbm(outer_basis[0, 0]), in_hbm(outer_tri[0, 0]))
    chips = lax.axis_size("group") * lax.axis_size("chip")
    blocks = terms.reshape(chips, 8, TILE)
    swapped = lax.all_to_all(blocks, ("group", "chip"), 0, 0, tiled=True)
    columns = pl.pallas_call(
        sum_kernel,
        out_shape=jax.ShapeDtypeStruct((half // chips, width), BF16),
        in_specs=[VMEM],
        out_specs=VMEM,
        compiler_params=pltpu.CompilerParams(vmem_limit_bytes=8 * 2**20),
    )(swapped)
    return columns.T


def solution(mesh):
    groups, leaves = mesh.devices.shape
    fine = Mesh(mesh.devices.reshape(groups, leaves // 2, 2), ("group", "chip", "core"))
    every = ("group", "chip", "core")
    leaf = ("chip", "core")
    placed = (
        P(every, None),
        P(every, None),
        P(every, None, None),
        P("group", leaf, None, None, None),
        P("group", leaf, None, None, None),
        P("group", leaf, None, None, None),
        P("group", leaf, None, None, None),
    )
    return jax.shard_map(
        per_device, mesh=fine, in_specs=placed, out_specs=P(None, every), check_vma=False
    )
```

```python
import functools

import jax
import jax.numpy as jnp
from jax import lax
from jax.experimental import pallas as pl
from jax.experimental.pallas import tpu as pltpu
from jax.sharding import Mesh, PartitionSpec as P

TILE = 256
UNITS = 2
GROUPS = (96, 80, 80)
F32 = jnp.float32
BF16 = jnp.bfloat16
VMEM = pl.BlockSpec(memory_space=pltpu.VMEM)
HBM = pl.BlockSpec(memory_space=pltpu.HBM)


def pair(rows):
    high = rows.astype(BF16)
    return high, (rows - high.astype(F32)).astype(BF16)


def pick_rows(side, half):
    row = lax.broadcasted_iota(jnp.int32, (half, 2 * half), 0)
    column = lax.broadcasted_iota(jnp.int32, (half, 2 * half), 1)
    wanted = (row // 4) * 8 + side * 4 + row % 4
    return jnp.where(column == wanted, 1.0, 0.0).astype(BF16)


def tile(index):
    return slice(index * TILE, (index + 1) * TILE)


def by_columns(depth):
    return lambda unit, group: [(unit, block) for block in range(depth)]


def triangle_plan(unit, group):
    return [(unit, block) for block in range(unit + 1)]


def even_triangle_plan(unit, group):
    if group == 1:
        return [(0, 0), (1, 0), (1, 1)] if unit == 0 else []
    return [(0, 0)] if unit == 0 else [(1, 0), (1, 1)]


def run_stages(stages, lhs, sums, spare):
    groups = len(GROUPS)
    slots = []
    for index, (plan, _, _) in enumerate(stages):
        for group in range(groups):
            rounds = max(len(plan(unit, group)) for unit in range(UNITS))
            slots += [(index, group, at) for at in range(rounds)]

    def depth_of(unit, slot):
        index, group, at = slot
        order = stages[index][0](unit, group)
        order = order[::-1] if group % 2 else order
        return order[at] if at < len(order) else None

    loads = [[] for _ in range(UNITS)]
    load_at = [{} for _ in range(UNITS)]
    for unit in range(UNITS):
        held = None
        for position, slot in enumerate(slots):
            depth = depth_of(unit, slot)
            if depth is not None and (slot[0], depth) != held:
                held = (slot[0], depth)
                load_at[unit][position] = len(loads[unit])
                loads[unit].append(held)
    pushed = [0] * UNITS

    def push(unit, count):
        while pushed[unit] < min(count, len(loads[unit])):
            index, product = loads[unit][pushed[unit]]
            matrix, transpose = stages[index][1](*product)
            pltpu.matmul_push_rhs(matrix, pushed[unit] % 2, unit, transpose=transpose)
            pushed[unit] += 1

    def outs_of(index, unit, group):
        return sorted({product[0] for product in stages[index][0](unit, group)})

    def total_of(index, unit, group, out):
        return (sums, spare)[outs_of(index, unit, group).index(out)][unit][group]

    rows = {}
    waiting = [(index, group) for index in range(len(stages)) for group in range(groups)]

    def finish():
        index, group = waiting.pop(0)
        tiles = {}
        for unit in range(UNITS):
            for out in outs_of(index, unit, group):
                tiles[out] = pltpu.matmul_pop(total_of(index, unit, group, out))
        rows[index + 1, group] = stages[index][2](group, [tiles[out] for out in sorted(tiles)])

    for position, slot in enumerate(slots):
        while slot[:2] not in rows:
            if slot[0]:
                finish()
            else:
                rows[slot[:2]] = lhs(slot[1])
        for part in range(len(rows[slot[:2]][0])):
            for unit in range(UNITS):
                depth = depth_of(unit, slot)
                if depth is None:
                    continue
                load = load_at[unit].get(position) if part == 0 else None
                if load is not None:
                    push(unit, load + 1)
                pltpu.matmul_acc_lhs(
                    total_of(*slot[:1], unit, slot[1], depth[0]),
                    rows[slot[:2]][depth[1]][part],
                    load_staged_rhs=None if load is None else load % 2,
                )
                if load is not None:
                    push(unit, load + 2)
    while waiting:
        finish()


def with_sums(body, kinds=1):
    def scoped(*flat):
        flat = iter(flat)
        body(*[[[next(flat) for _ in GROUPS] for _ in range(UNITS)] for _ in range(kinds)])

    pl.run_scoped(
        scoped,
        *[
            pltpu.ACC(unit)((count, TILE), F32)
            for _ in range(kinds)
            for unit in range(UNITS)
            for count in GROUPS
        ],
    )


def pairs(group, tiles):
    return [pair(values) for values in tiles]


def once(copies):
    done = set()

    def ready(index):
        if index not in done:
            done.add(index)
            copies[index].wait()

    return ready


def fetch(sources, targets, sems):
    copies = [
        pltpu.make_async_copy(source, target, sems.at[index])
        for index, (source, target) in enumerate(zip(sources, targets, strict=True))
    ]
    for copy in copies:
        copy.start()
    return copies


def run_leaf(side, x_ref, v_ref, f_ref, out_ref, ready):
    blocks = x_ref.shape[0] // TILE
    offsets = [sum(GROUPS[:group]) for group in range(len(GROUPS))]
    spans = [slice(start, start + count) for start, count in zip(offsets, GROUPS, strict=True)]
    pick = pick_rows(side, out_ref.shape[0])

    def body(first, second, sums, late):
        pushed = [0] * UNITS

        def push(unit, count):
            while pushed[unit] < min(count, 2 * blocks):
                load = pushed[unit]
                if load < blocks:
                    out, depth = UNITS * (load // 2) + unit, load % 2
                    ready(out)
                    matrix = x_ref[tile(out), tile(depth)]
                else:
                    ready(load)
                    matrix = v_ref[tile(load - blocks), tile(unit)]
                pltpu.matmul_push_rhs(matrix, load % 2, unit, transpose=load < blocks)
                pushed[unit] += 1

        def product(load, totals, rows):
            for unit in range(UNITS):
                push(unit, load + 1)
                for group, part in enumerate(rows):
                    pltpu.matmul_acc_lhs(
                        totals[unit][group], part, load_staged_rhs=None if group else load % 2
                    )
                push(unit, load + 2)

        for load in range(blocks):
            totals = first if load < 2 else second
            product(load, totals, [pick[span, tile(load % 2)] for span in spans])
        tops = []
        for index, totals in enumerate((first, second)):
            panel = [
                [pltpu.matmul_pop(totals[unit][group]) for group in range(len(GROUPS))]
                for unit in range(UNITS)
            ]
            if index == 0:
                tops = panel
            for unit in range(UNITS):
                rows = [values.astype(BF16) for values in panel[unit]]
                product(blocks + UNITS * index + unit, sums, rows)

        def projected(group):
            return pairs(group, [pltpu.matmul_pop(sums[unit][group]) for unit in range(UNITS)])

        def triangle(out, depth):
            ready(2 * blocks)
            return f_ref[tile(depth), tile(out)], False

        def top(out, depth):
            return v_ref[tile(out), tile(depth)], True

        def finish(group, tiles):
            for out, values in enumerate(tiles):
                out_ref[pl.ds(offsets[group], GROUPS[group]), tile(out)] = tops[out][group] - values

        run_stages(
            [(even_triangle_plan, triangle, pairs), (by_columns(2), top, finish)], projected, late, first
        )

    with_sums(body, 4)


def send_kernel(x_hbm, v_hbm, f_hbm, ib_hbm, it_hbm, out_ref, x_ref, v_ref, f_ref, wv_ref, wf_ref, sems):
    tiles = [pl.ds(block * TILE, TILE) for block in range(x_hbm.shape[0] // TILE)]
    sources = [ref.at[span] for ref in (x_hbm, v_hbm) for span in tiles] + [f_hbm]
    targets = [ref.at[span] for ref in (x_ref, v_ref) for span in tiles] + [f_ref]
    for level in range(wv_ref.shape[0]):
        sources += [ib_hbm.at[level], it_hbm.at[level]]
        targets += [wv_ref.at[level], wf_ref.at[level]]
    copies = fetch(sources, targets, sems)
    side = 1 - lax.axis_index("core")
    run_leaf(side, x_ref, v_ref, f_ref, out_ref, once(copies))
    for copy in copies[2 * len(tiles) + 1 :]:
        copy.wait()


def keep_kernel(x_ref, v_ref, f_ref, out_ref):
    run_leaf(lax.axis_index("core"), x_ref, v_ref, f_ref, out_ref, lambda index: None)


def chain_kernel(
    own_ref, other_ref, wv_ref, wf_ref, ib_hbm, it_hbm, ob_hbm, ot_hbm, out_ref, v_buf, f_buf, sems
):
    width = own_ref.shape[1]
    offsets = [sum(GROUPS[:group]) for group in range(len(GROUPS))]
    early, inner, outer = wv_ref.shape[0], ib_hbm.shape[0], ob_hbm.shape[0]
    sources = []
    for level in range(early, inner):
        sources += [ib_hbm.at[level], it_hbm.at[level]]
    for level in range(outer):
        sources += [ob_hbm.at[level], ot_hbm.at[level]]
    late = inner + outer - early
    targets = [buf.at[index] for index in range(late) for buf in (v_buf, f_buf)]
    arrived = once(fetch(sources, targets, sems))
    core = lax.axis_index("core")
    place = lax.axis_index("group") * lax.axis_size("chip") + lax.axis_index("chip")
    summit = [None] * len(GROUPS)

    def level_stages(level):
        basis_ref, tri_ref, at = (
            (wv_ref, wf_ref, level) if level < early else (v_buf, f_buf, level - early)
        )
        bit = jnp.right_shift(place, level - 1) & 1 if level else 0
        first = bit * width

        def basis(out, depth):
            if level >= early:
                arrived(2 * at)
            start = pl.multiple_of(first + depth * TILE, TILE)
            return basis_ref[at, pl.ds(start, TILE), tile(out)], False

        def triangle(out, depth):
            if level >= early:
                arrived(2 * at + 1)
            return tri_ref[at, tile(depth), tile(out)], False

        def top(out, depth):
            return basis_ref[at, tile(out), tile(depth)], True

        def after(group, tiles):
            base = summit[group]
            if level:
                base = [jnp.where(bit == 0, values, 0.0) for values in base]
            summit[group] = [kept - values for kept, values in zip(base, tiles, strict=True)]
            return pairs(group, summit[group])

        def last(group, tiles):
            after(group, tiles)
            left, right = summit[group]
            count = GROUPS[group]
            upper = lax.broadcasted_iota(jnp.int32, (count, TILE), 0) % 8 < 4
            even = jnp.where(upper, left, pltpu.roll(right, 4, 0))
            odd = jnp.where(upper, pltpu.roll(left, count - 4, 0), right)
            for index, values in enumerate((even, odd)):
                at = pl.ds(offsets[group] // 8, count // 8)
                out_ref[at, index] = values.reshape(count // 8, 8, TILE)

        end = last if level == inner + outer - 1 else after
        return [
            (by_columns(2 if level else 4), basis, pairs),
            (triangle_plan, triangle, pairs),
            (by_columns(2), top, end),
        ]

    def lhs(group):
        at = pl.ds(offsets[group], GROUPS[group])
        own = [own_ref[at, tile(out)] for out in range(2)]
        other = [other_ref[at, tile(out)] for out in range(2)]
        summit[group] = [jnp.where(core == 0, a, b) for a, b in zip(own, other, strict=True)]
        upper = [jnp.where(core == 0, b, a) for a, b in zip(own, other, strict=True)]
        return pairs(group, summit[group] + upper)

    stages = [stage for level in range(inner + outer) for stage in level_stages(level)]
    with_sums(lambda sums, spare: run_stages(stages, lhs, sums, spare), 2)


def in_hbm(array):
    return pltpu.with_memory_space_constraint(array, pltpu.HBM)


def sum_kernel(terms_ref, out_ref):
    total = jnp.sum(terms_ref[...], axis=0)
    out_ref[...] = jnp.concatenate([total[:4], total[4:]], axis=1).astype(BF16)


def estimate(units, mebibytes):
    return pl.CostEstimate(
        flops=units * 2 * 512**3, bytes_accessed=mebibytes * 2**20, transcendentals=0
    )


def per_device(matrix, leaf_basis, leaf_tri, inner_basis, inner_tri, outer_basis, outer_tri):
    rows, width = leaf_basis.shape
    half = matrix.shape[1] // 2
    inner, outer = inner_basis.shape[2], outer_basis.shape[2]
    ahead = 2
    trees = (in_hbm(inner_basis[0, 0]), in_hbm(inner_tri[0, 0]))

    def basis_of(levels):
        return jax.ShapeDtypeStruct((levels, rows, width), BF16)

    def tri_of(levels):
        return jax.ShapeDtypeStruct((levels, width, width), BF16)

    summit = jax.ShapeDtypeStruct((half, width), F32)
    sent, x, v, f, wv, wf = pl.pallas_call(
        send_kernel,
        out_shape=(
            summit,
            jax.ShapeDtypeStruct(matrix.shape, BF16),
            jax.ShapeDtypeStruct((rows, width), BF16),
            jax.ShapeDtypeStruct((width, width), BF16),
            basis_of(ahead),
            tri_of(ahead),
        ),
        in_specs=[HBM] * 5,
        out_specs=(VMEM,) * 6,
        scratch_shapes=[pltpu.SemaphoreType.DMA((2 * rows // TILE + 1 + 2 * ahead,))],
        cost_estimate=estimate(4, 4),
        compiler_params=pltpu.CompilerParams(vmem_limit_bytes=16 * 2**20),
    )(in_hbm(matrix), in_hbm(leaf_basis), in_hbm(leaf_tri[0]), *trees)
    other = lax.ppermute(sent, "core", [(0, 1), (1, 0)])
    own = pl.pallas_call(
        keep_kernel,
        out_shape=summit,
        in_specs=[VMEM] * 3,
        out_specs=VMEM,
        cost_estimate=estimate(4, 4),
        compiler_params=pltpu.CompilerParams(vmem_limit_bytes=16 * 2**20),
    )(x, v, f)
    late = inner + outer - ahead
    terms = pl.pallas_call(
        chain_kernel,
        out_shape=jax.ShapeDtypeStruct((half // 8, 2, 8, TILE), F32),
        in_specs=[VMEM] * 4 + [HBM] * 4,
        out_specs=VMEM,
        scratch_shapes=[
            pltpu.VMEM((late, rows, width), BF16),
            pltpu.VMEM((late, width, width), BF16),
            pltpu.SemaphoreType.DMA((2 * late,)),
        ],
        cost_estimate=estimate(22, 12),
        compiler_params=pltpu.CompilerParams(vmem_limit_bytes=24 * 2**20),
    )(own, other, wv, wf, *trees, in_hbm(outer_basis[0, 0]), in_hbm(outer_tri[0, 0]))
    chips = lax.axis_size("group") * lax.axis_size("chip")
    blocks = terms.reshape(chips, 8, TILE)
    swapped = lax.all_to_all(blocks, ("group", "chip"), 0, 0, tiled=True)
    columns = pl.pallas_call(
        sum_kernel,
        out_shape=jax.ShapeDtypeStruct((half // chips, width), BF16),
        in_specs=[VMEM],
        out_specs=VMEM,
        compiler_params=pltpu.CompilerParams(vmem_limit_bytes=8 * 2**20),
    )(swapped)
    return columns.T


def solution(mesh):
    groups, leaves = mesh.devices.shape
    fine = Mesh(mesh.devices.reshape(groups, leaves // 2, 2), ("group", "chip", "core"))
    every = ("group", "chip", "core")
    leaf = ("chip", "core")
    placed = (
        P(every, None),
        P(every, None),
        P(every, None, None),
        P("group", leaf, None, None, None),
        P("group", leaf, None, None, None),
        P("group", leaf, None, None, None),
        P("group", leaf, None, None, None),
    )
    return jax.shard_map(
        per_device, mesh=fine, in_specs=placed, out_specs=P(None, every), check_vma=False
    )
```

```python
import functools

import jax
import jax.numpy as jnp
from jax import lax
from jax.experimental import pallas as pl
from jax.experimental.pallas import tpu as pltpu
from jax.sharding import Mesh, PartitionSpec as P

TILE = 256
UNITS = 2
GROUPS = (80, 80, 96)
F32 = jnp.float32
BF16 = jnp.bfloat16
VMEM = pl.BlockSpec(memory_space=pltpu.VMEM)
HBM = pl.BlockSpec(memory_space=pltpu.HBM)


def pair(rows):
    high = rows.astype(BF16)
    return high, (rows - high.astype(F32)).astype(BF16)


def pick_rows(side, half):
    row = lax.broadcasted_iota(jnp.int32, (half, 2 * half), 0)
    column = lax.broadcasted_iota(jnp.int32, (half, 2 * half), 1)
    wanted = (row // 4) * 8 + side * 4 + row % 4
    return jnp.where(column == wanted, 1.0, 0.0).astype(BF16)


def tile(index):
    return slice(index * TILE, (index + 1) * TILE)


def by_columns(depth):
    return lambda unit, group: [(unit, block) for block in range(depth)]


def triangle_plan(unit, group):
    return [(unit, block) for block in range(unit + 1)]


def even_triangle_plan(unit, group):
    if group == 1:
        return [(0, 0), (1, 0), (1, 1)] if unit == 0 else []
    return [(0, 0)] if unit == 0 else [(1, 0), (1, 1)]


def run_stages(stages, lhs, sums, spare):
    groups = len(GROUPS)
    slots = []
    for index, (plan, _, _) in enumerate(stages):
        for group in range(groups):
            rounds = max(len(plan(unit, group)) for unit in range(UNITS))
            slots += [(index, group, at) for at in range(rounds)]

    def depth_of(unit, slot):
        index, group, at = slot
        order = stages[index][0](unit, group)
        order = order[::-1] if group % 2 else order
        return order[at] if at < len(order) else None

    loads = [[] for _ in range(UNITS)]
    load_at = [{} for _ in range(UNITS)]
    for unit in range(UNITS):
        held = None
        for position, slot in enumerate(slots):
            depth = depth_of(unit, slot)
            if depth is not None and (slot[0], depth) != held:
                held = (slot[0], depth)
                load_at[unit][position] = len(loads[unit])
                loads[unit].append(held)
    pushed = [0] * UNITS

    def push(unit, count):
        while pushed[unit] < min(count, len(loads[unit])):
            index, product = loads[unit][pushed[unit]]
            matrix, transpose = stages[index][1](*product)
            pltpu.matmul_push_rhs(matrix, pushed[unit] % 2, unit, transpose=transpose)
            pushed[unit] += 1

    def outs_of(index, unit, group):
        return sorted({product[0] for product in stages[index][0](unit, group)})

    def total_of(index, unit, group, out):
        return (sums, spare)[outs_of(index, unit, group).index(out)][unit][group]

    rows = {}
    waiting = [(index, group) for index in range(len(stages)) for group in range(groups)]

    def finish():
        index, group = waiting.pop(0)
        tiles = {}
        for unit in range(UNITS):
            for out in outs_of(index, unit, group):
                tiles[out] = pltpu.matmul_pop(total_of(index, unit, group, out))
        rows[index + 1, group] = stages[index][2](group, [tiles[out] for out in sorted(tiles)])

    for position, slot in enumerate(slots):
        while slot[:2] not in rows:
            if slot[0]:
                finish()
            else:
                rows[slot[:2]] = lhs(slot[1])
        for part in range(len(rows[slot[:2]][0])):
            for unit in range(UNITS):
                depth = depth_of(unit, slot)
                if depth is None:
                    continue
                load = load_at[unit].get(position) if part == 0 else None
                if load is not None:
                    push(unit, load + 1)
                pltpu.matmul_acc_lhs(
                    total_of(*slot[:1], unit, slot[1], depth[0]),
                    rows[slot[:2]][depth[1]][part],
                    load_staged_rhs=None if load is None else load % 2,
                )
                if load is not None:
                    push(unit, load + 2)
    while waiting:
        finish()


def with_sums(body, kinds=1):
    def scoped(*flat):
        flat = iter(flat)
        body(*[[[next(flat) for _ in GROUPS] for _ in range(UNITS)] for _ in range(kinds)])

    pl.run_scoped(
        scoped,
        *[
            pltpu.ACC(unit)((count, TILE), F32)
            for _ in range(kinds)
            for unit in range(UNITS)
            for count in GROUPS
        ],
    )


def pairs(group, tiles):
    return [pair(values) for values in tiles]


def once(copies):
    done = set()

    def ready(index):
        if index not in done:
            done.add(index)
            copies[index].wait()

    return ready


def fetch(sources, targets, sems):
    copies = [
        pltpu.make_async_copy(source, target, sems.at[index])
        for index, (source, target) in enumerate(zip(sources, targets, strict=True))
    ]
    for copy in copies:
        copy.start()
    return copies


def run_leaf(side, x_ref, v_ref, f_ref, out_ref, ready):
    blocks = x_ref.shape[0] // TILE
    offsets = [sum(GROUPS[:group]) for group in range(len(GROUPS))]
    spans = [slice(start, start + count) for start, count in zip(offsets, GROUPS, strict=True)]
    pick = pick_rows(side, out_ref.shape[0])

    def body(first, second, sums, late):
        pushed = [0] * UNITS

        def push(unit, count):
            while pushed[unit] < min(count, 2 * blocks):
                load = pushed[unit]
                if load < blocks:
                    out, depth = UNITS * (load // 2) + unit, load % 2
                    ready(out)
                    matrix = x_ref[tile(out), tile(depth)]
                else:
                    ready(load)
                    matrix = v_ref[tile(load - blocks), tile(unit)]
                pltpu.matmul_push_rhs(matrix, load % 2, unit, transpose=load < blocks)
                pushed[unit] += 1

        def product(load, totals, rows):
            for unit in range(UNITS):
                push(unit, load + 1)
                for group, part in enumerate(rows):
                    pltpu.matmul_acc_lhs(
                        totals[unit][group], part, load_staged_rhs=None if group else load % 2
                    )
                push(unit, load + 2)

        for load in range(blocks):
            totals = first if load < 2 else second
            product(load, totals, [pick[span, tile(load % 2)] for span in spans])
        tops = []
        for index, totals in enumerate((first, second)):
            panel = [
                [pltpu.matmul_pop(totals[unit][group]) for group in range(len(GROUPS))]
                for unit in range(UNITS)
            ]
            if index == 0:
                tops = panel
            for unit in range(UNITS):
                rows = [values.astype(BF16) for values in panel[unit]]
                product(blocks + UNITS * index + unit, sums, rows)

        def projected(group):
            return pairs(group, [pltpu.matmul_pop(sums[unit][group]) for unit in range(UNITS)])

        def triangle(out, depth):
            ready(2 * blocks)
            return f_ref[tile(depth), tile(out)], False

        def top(out, depth):
            return v_ref[tile(out), tile(depth)], True

        def finish(group, tiles):
            for out, values in enumerate(tiles):
                out_ref[pl.ds(offsets[group], GROUPS[group]), tile(out)] = tops[out][group] - values

        run_stages(
            [(even_triangle_plan, triangle, pairs), (by_columns(2), top, finish)], projected, late, first
        )

    with_sums(body, 4)


def send_kernel(x_hbm, v_hbm, f_hbm, ib_hbm, it_hbm, out_ref, x_ref, v_ref, f_ref, wv_ref, wf_ref, sems):
    tiles = [pl.ds(block * TILE, TILE) for block in range(x_hbm.shape[0] // TILE)]
    sources = [ref.at[span] for ref in (x_hbm, v_hbm) for span in tiles] + [f_hbm]
    targets = [ref.at[span] for ref in (x_ref, v_ref) for span in tiles] + [f_ref]
    for level in range(wv_ref.shape[0]):
        sources += [ib_hbm.at[level], it_hbm.at[level]]
        targets += [wv_ref.at[level], wf_ref.at[level]]
    copies = fetch(sources, targets, sems)
    side = 1 - lax.axis_index("core")
    run_leaf(side, x_ref, v_ref, f_ref, out_ref, once(copies))
    for copy in copies[2 * len(tiles) + 1 :]:
        copy.wait()


def keep_kernel(x_ref, v_ref, f_ref, out_ref):
    run_leaf(lax.axis_index("core"), x_ref, v_ref, f_ref, out_ref, lambda index: None)


def chain_kernel(
    own_ref, other_ref, wv_ref, wf_ref, ib_hbm, it_hbm, ob_hbm, ot_hbm, out_ref, v_buf, f_buf, sems
):
    width = own_ref.shape[1]
    offsets = [sum(GROUPS[:group]) for group in range(len(GROUPS))]
    early, inner, outer = wv_ref.shape[0], ib_hbm.shape[0], ob_hbm.shape[0]
    sources = []
    for level in range(early, inner):
        sources += [ib_hbm.at[level], it_hbm.at[level]]
    for level in range(outer):
        sources += [ob_hbm.at[level], ot_hbm.at[level]]
    late = inner + outer - early
    targets = [buf.at[index] for index in range(late) for buf in (v_buf, f_buf)]
    arrived = once(fetch(sources, targets, sems))
    core = lax.axis_index("core")
    place = lax.axis_index("group") * lax.axis_size("chip") + lax.axis_index("chip")
    summit = [None] * len(GROUPS)

    def level_stages(level):
        basis_ref, tri_ref, at = (
            (wv_ref, wf_ref, level) if level < early else (v_buf, f_buf, level - early)
        )
        bit = jnp.right_shift(place, level - 1) & 1 if level else 0
        first = bit * width

        def basis(out, depth):
            if level >= early:
                arrived(2 * at)
            start = pl.multiple_of(first + depth * TILE, TILE)
            return basis_ref[at, pl.ds(start, TILE), tile(out)], False

        def triangle(out, depth):
            if level >= early:
                arrived(2 * at + 1)
            return tri_ref[at, tile(depth), tile(out)], False

        def top(out, depth):
            return basis_ref[at, tile(out), tile(depth)], True

        def after(group, tiles):
            base = summit[group]
            if level:
                base = [jnp.where(bit == 0, values, 0.0) for values in base]
            summit[group] = [kept - values for kept, values in zip(base, tiles, strict=True)]
            return pairs(group, summit[group])

        def last(group, tiles):
            after(group, tiles)
            left, right = summit[group]
            count = GROUPS[group]
            upper = lax.broadcasted_iota(jnp.int32, (count, TILE), 0) % 8 < 4
            even = jnp.where(upper, left, pltpu.roll(right, 4, 0))
            odd = jnp.where(upper, pltpu.roll(left, count - 4, 0), right)
            for index, values in enumerate((even, odd)):
                at = pl.ds(offsets[group] // 8, count // 8)
                out_ref[at, index] = values.reshape(count // 8, 8, TILE)

        end = last if level == inner + outer - 1 else after
        return [
            (by_columns(2 if level else 4), basis, pairs),
            (triangle_plan, triangle, pairs),
            (by_columns(2), top, end),
        ]

    def lhs(group):
        at = pl.ds(offsets[group], GROUPS[group])
        own = [own_ref[at, tile(out)] for out in range(2)]
        other = [other_ref[at, tile(out)] for out in range(2)]
        summit[group] = [jnp.where(core == 0, a, b) for a, b in zip(own, other, strict=True)]
        upper = [jnp.where(core == 0, b, a) for a, b in zip(own, other, strict=True)]
        return pairs(group, summit[group] + upper)

    stages = [stage for level in range(inner + outer) for stage in level_stages(level)]
    with_sums(lambda sums, spare: run_stages(stages, lhs, sums, spare), 2)


def in_hbm(array):
    return pltpu.with_memory_space_constraint(array, pltpu.HBM)


def sum_kernel(terms_ref, out_ref):
    total = jnp.sum(terms_ref[...], axis=0)
    out_ref[...] = jnp.concatenate([total[:4], total[4:]], axis=1).astype(BF16)


def estimate(units, mebibytes):
    return pl.CostEstimate(
        flops=units * 2 * 512**3, bytes_accessed=mebibytes * 2**20, transcendentals=0
    )


def per_device(matrix, leaf_basis, leaf_tri, inner_basis, inner_tri, outer_basis, outer_tri):
    rows, width = leaf_basis.shape
    half = matrix.shape[1] // 2
    inner, outer = inner_basis.shape[2], outer_basis.shape[2]
    ahead = 2
    trees = (in_hbm(inner_basis[0, 0]), in_hbm(inner_tri[0, 0]))

    def basis_of(levels):
        return jax.ShapeDtypeStruct((levels, rows, width), BF16)

    def tri_of(levels):
        return jax.ShapeDtypeStruct((levels, width, width), BF16)

    summit = jax.ShapeDtypeStruct((half, width), F32)
    sent, x, v, f, wv, wf = pl.pallas_call(
        send_kernel,
        out_shape=(
            summit,
            jax.ShapeDtypeStruct(matrix.shape, BF16),
            jax.ShapeDtypeStruct((rows, width), BF16),
            jax.ShapeDtypeStruct((width, width), BF16),
            basis_of(ahead),
            tri_of(ahead),
        ),
        in_specs=[HBM] * 5,
        out_specs=(VMEM,) * 6,
        scratch_shapes=[pltpu.SemaphoreType.DMA((2 * rows // TILE + 1 + 2 * ahead,))],
        cost_estimate=estimate(4, 4),
        compiler_params=pltpu.CompilerParams(vmem_limit_bytes=16 * 2**20),
    )(in_hbm(matrix), in_hbm(leaf_basis), in_hbm(leaf_tri[0]), *trees)
    other = lax.ppermute(sent, "core", [(0, 1), (1, 0)])
    own = pl.pallas_call(
        keep_kernel,
        out_shape=summit,
        in_specs=[VMEM] * 3,
        out_specs=VMEM,
        cost_estimate=estimate(4, 4),
        compiler_params=pltpu.CompilerParams(vmem_limit_bytes=16 * 2**20),
    )(x, v, f)
    late = inner + outer - ahead
    terms = pl.pallas_call(
        chain_kernel,
        out_shape=jax.ShapeDtypeStruct((half // 8, 2, 8, TILE), F32),
        in_specs=[VMEM] * 4 + [HBM] * 4,
        out_specs=VMEM,
        scratch_shapes=[
            pltpu.VMEM((late, rows, width), BF16),
            pltpu.VMEM((late, width, width), BF16),
            pltpu.SemaphoreType.DMA((2 * late,)),
        ],
        cost_estimate=estimate(22, 12),
        compiler_params=pltpu.CompilerParams(vmem_limit_bytes=24 * 2**20),
    )(own, other, wv, wf, *trees, in_hbm(outer_basis[0, 0]), in_hbm(outer_tri[0, 0]))
    chips = lax.axis_size("group") * lax.axis_size("chip")
    blocks = terms.reshape(chips, 8, TILE)
    swapped = lax.all_to_all(blocks, ("group", "chip"), 0, 0, tiled=True)
    columns = pl.pallas_call(
        sum_kernel,
        out_shape=jax.ShapeDtypeStruct((half // chips, width), BF16),
        in_specs=[VMEM],
        out_specs=VMEM,
        compiler_params=pltpu.CompilerParams(vmem_limit_bytes=8 * 2**20),
    )(swapped)
    return columns.T


def solution(mesh):
    groups, leaves = mesh.devices.shape
    fine = Mesh(mesh.devices.reshape(groups, leaves // 2, 2), ("group", "chip", "core"))
    every = ("group", "chip", "core")
    leaf = ("chip", "core")
    placed = (
        P(every, None),
        P(every, None),
        P(every, None, None),
        P("group", leaf, None, None, None),
        P("group", leaf, None, None, None),
        P("group", leaf, None, None, None),
        P("group", leaf, None, None, None),
    )
    return jax.shard_map(
        per_device, mesh=fine, in_specs=placed, out_specs=P(None, every), check_vma=False
    )
```
